32 devices in a mesh: depth: 8 (over y, x, core), strip: 4 (over z).
Axes of the slice: x: 2, y: 2, z: 4, core: 2. Of those that a mesh axis runs over, the one named last changes fastest.
Arguments:
- arrivals: float32 [8, 1, 4, 128, 128], P('depth', None, None, 'strip'), may hold values from -6 to 6
- feed: float32 [3, 1, 4, 128, 128], P(None, None, None, 'strip'), may hold values from -6 to 6
- velocity_index: int32 [16, 128, 128], P('depth', 'strip'), may hold values from 0 to 31
- offsets: int32 [16], replicated, may hold values from -8 to 8, as said below
- coef_table: float32 [11, 9, 2, 1, 32], replicated, may hold values from -1.8 to 1.8
Outputs:
- image: float32 [16, 16, 128, 128], P('depth', None, 'strip')
- outflow: float32 [8, 1, 4, 128, 128], P('depth', None, None, 'strip')
The draws below stay inside these ranges and needn't reach their ends.
Inputs may be any that keep to these rules, and one draw needn't show every extreme that they name: The 16 offsets are distinct, and both -8 and 8 occur among them.
All inputs are finite; a program needn't handle non-finite values.
Results may differ from the reference program's by a relative error of at most 0.00025.
Values sent between devices are 32-bit elements; how exact they have to be, the bound alone decides.
No kernel may reach another device: no remote copies, remote signals or barrier semaphores. Data moves between devices by JAX's collectives and lax.ppermute only.
A program may use at most 64 MiB of HBM per device.

```python
import jax
import jax.numpy as jnp
from jax import lax

NY = 128
F = 1
LEVELS = 32
NOFF = 16
ORDER = 8
HMAX = 8
TICKS = 4
LAYERS = 2
NSEC = 8
NZ = 16
NX = 128
NB = 11


def draw_offsets(key, part):
    inner = jax.random.permutation(jax.random.fold_in(key, 11), 2 * HMAX - 1).astype(jnp.int32) - (HMAX - 1)
    ends = jnp.array([-HMAX, HMAX], jnp.int32)
    chosen = jnp.concatenate([ends, inner[:NOFF - 2]])
    shuffle = jax.random.permutation(jax.random.fold_in(key, 23), NOFF)
    return chosen[shuffle].astype(jnp.int32)


def set_ends(values, own_key, low, high):
    longest = values.shape.index(max(values.shape))
    spots = []
    for shift in (0, 1):
        where = [jax.random.randint(jax.random.fold_in(own_key, axis), (), 0, length) for axis, length in enumerate(values.shape)]
        where[longest] = (where[longest] + shift) % values.shape[longest]
        spots.append(tuple(where))
    return values.at[spots[0]].set(low).at[spots[1]].set(high)


def block_levels(key, dims, pieces, least, high):
    loudness, own = 1.0, jax.random.fold_in(key, 6)
    for position, blocks in pieces:
        draws = jnp.exp(jax.random.uniform(jax.random.fold_in(own, position), (blocks,), jnp.float32, least / len(pieces), high / len(pieces)))
        loudness = loudness * jnp.repeat(draws, dims[position] // blocks).reshape([-1 if axis == position else 1 for axis in range(len(dims))])
    return loudness


def noise(key, shape, scale, most, cuts=(), kind=jnp.bfloat16):
    loudness = block_levels(key, shape, cuts, -0.22, 0.18) if cuts else 1.0
    values = jax.random.normal(key, shape, jnp.float32) * scale * loudness
    return jnp.minimum(jnp.maximum(values, -most), most).astype(kind)


def setup_inputs(seed: int = 0) -> dict:
    keys = jax.random.split(jax.random.key(seed), 6)
    return {
        "arrivals": noise(keys[0], (NSEC, F, 4, NX, NY), 1.0, 6.0, ((0, 8), (3, 4)), jnp.float32),
        "feed": noise(keys[1], (TICKS - 1, F, 4, NX, NY), 1.0, 6.0, ((3, 4),), jnp.float32),
        "velocity_index": set_ends(jax.random.randint(keys[2], (NZ, NX, NY), 0, LEVELS), jax.random.fold_in(keys[2], 1), 0, LEVELS - 1).astype(jnp.int32),
        "offsets": draw_offsets(jax.random.fold_in(keys[5], 71), 0),
        "coef_table": noise(keys[4], (NB, ORDER + 1, 2, F, LEVELS), 0.3, 1.8, (), jnp.float32),
    }


def lateral(field):
    lead = [(0, 0)] * (field.ndim - 2)
    along_y = jnp.pad(field, lead + [(0, 0), (1, 1)])
    smooth_y = field + 0.5 * (along_y[..., 2:] + along_y[..., :-2])
    along_x = jnp.pad(smooth_y, lead + [(1, 1), (0, 0)])
    smooth_x = smooth_y + 0.5 * (along_x[..., 2:, :] + along_x[..., :-2, :])
    return 0.5 * smooth_x - field


def weighted(total, term, coef_re, coef_im):
    source_re = term[..., 0, :, :]
    source_im = term[..., 1, :, :]
    receiver_re = term[..., 2, :, :]
    receiver_im = term[..., 3, :, :]
    piece = jnp.stack([coef_re * source_re - coef_im * source_im,
                       coef_re * source_im + coef_im * source_re,
                       coef_re * receiver_re + coef_im * receiver_im,
                       coef_re * receiver_im - coef_im * receiver_re], axis=-3)
    return total + piece


def extrapolate(state, table, levels):
    def pick(order):
        chosen_part = table[:, order]
        chosen = jax.vmap(lambda rows, cells: jnp.take(rows, cells, axis=-1))(chosen_part, levels)
        return chosen[:, 0], chosen[:, 1]

    earlier = state
    first_re, first_im = pick(0)
    total = weighted(jnp.zeros_like(state), state, first_re, first_im)
    current = lateral(state)
    second_re, second_im = pick(1)
    total = weighted(total, current, second_re, second_im)
    for order in range(2, ORDER + 1):
        following = 2.0 * lateral(current) - earlier
        earlier, current = current, following
        coef_re, coef_im = pick(order)
        total = weighted(total, current, coef_re, coef_im)
    return total


def image_terms(state, offsets):
    padded = jnp.pad(state, [(0, 0)] * 3 + [(HMAX, HMAX), (0, 0)])
    width = state.shape[3]
    rows = []
    for index in range(NOFF):
        offset = offsets[index]
        source = lax.dynamic_slice_in_dim(padded, (HMAX - offset).astype(jnp.int32), width, axis=3)
        receiver = lax.dynamic_slice_in_dim(padded, (HMAX + offset).astype(jnp.int32), width, axis=3)
        rows.append(jnp.sum(source[:, :, 0] * receiver[:, :, 2] + source[:, :, 1] * receiver[:, :, 3], axis=1))
    return jnp.stack(rows, axis=1)


def reference(arrivals, feed, velocity_index, offsets, coef_table):
    state = arrivals
    sections = jnp.arange(NSEC, dtype=jnp.int32)
    levels_all = velocity_index.reshape(NSEC, LAYERS, NX, NY)
    image = jnp.zeros((NSEC, LAYERS, NOFF, NX, NY), jnp.float32)
    for tick in range(TICKS):
        table = coef_table[(tick - sections + NSEC - 1).astype(jnp.int32)]
        for row in range(LAYERS):
            state = extrapolate(state, table, levels_all[:, row])
            image = image.at[:, row].add(image_terms(state, offsets))
        if tick + 1 < TICKS:
            state = jnp.concatenate([feed[tick][None], state[:-1]], axis=0)
    return image.reshape(NSEC * LAYERS, NOFF, NX, NY), state
```

```python
import functools

import jax
import jax.numpy as jnp
from jax import lax
from jax.experimental import pallas as pl
from jax.experimental.pallas import tpu as pltpu
from jax.sharding import PartitionSpec as P

SUB = 8
LANES = 128
VMEM = pl.BlockSpec(memory_space=pltpu.VMEM)
SMEM = pl.BlockSpec(memory_space=pltpu.SMEM)


def layer_step(terms, smooth, table_ref, table_row, velocity_ref, layer, start, rows, orders, wides, left, right):
    tiles = rows // SUB
    comps = terms.shape[1]
    zero = jnp.zeros((SUB, LANES), jnp.float32)
    base = pl.multiple_of(start + SUB, SUB)

    def rows_of(order, comp, tile):
        return terms[order, comp, pl.ds(pl.multiple_of(base + tile * SUB, SUB), SUB), :]

    for comp in range(comps):
        smooth[comp, 0:SUB, :] = zero
        smooth[comp, SUB + rows:2 * SUB + rows, :] = zero
    for order in range(orders):
        for comp in range(comps):
            held = {}

            def along_y(tile):
                cells = rows_of(order, comp, tile)
                wide = cells + (left * pltpu.roll(cells, 1, 1) + right * pltpu.roll(cells, LANES - 1, 1))
                smooth[comp, SUB + tile * SUB:2 * SUB + tile * SUB, :] = wide
                held[tile] = (cells, wide)

            def along_x(tile):
                cells, wide = held.pop(tile)
                low = SUB + tile * SUB
                sides = smooth[comp, low - 1:low - 1 + SUB, :] + smooth[comp, low + 1:low + 1 + SUB, :]
                both = wide + 0.5 * sides
                if order == 0:
                    following = 0.5 * both - cells
                else:
                    following = (both - rows_of(order - 1, comp, tile)) - (cells + cells)
                terms[order + 1, comp, pl.ds(pl.multiple_of(base + tile * SUB, SUB), SUB), :] = following

            along_y(0)
            for tile in range(1, tiles):
                along_y(tile)
                along_x(tile - 1)
            along_x(tiles - 1)
    for tile in range(tiles):
        index = velocity_ref[layer, pl.ds(pl.multiple_of(start + tile * SUB, SUB), SUB), :]
        total = [None] * comps
        for order in range(orders + 1):
            parts = []
            for part in range(2):
                row = table_ref[pl.ds(table_row + 2 * order + part, 1), :]
                parts.append(jnp.take_along_axis(jnp.broadcast_to(row, (SUB, LANES)), index, axis=1, mode="promise_in_bounds"))
            re, im = parts
            cells = [rows_of(order, comp, tile) for comp in range(comps)]
            pieces = [re * cells[0] - im * cells[1], re * cells[1] + im * cells[0],
                      re * cells[2] + im * cells[3], re * cells[3] - im * cells[2]]
            total = [piece if old is None else old + piece for old, piece in zip(total, pieces)]
        for comp in range(comps):
            terms[0, comp, pl.ds(pl.multiple_of(base + tile * SUB, SUB), SUB), :] = total[comp]


def lane_weights():
    lane = lax.broadcasted_iota(jnp.int32, (SUB, LANES), 1)
    left = jnp.where(lane == 0, 0.0, 0.5).astype(jnp.float32)
    right = jnp.where(lane == LANES - 1, 0.0, 0.5).astype(jnp.float32)
    return left, right


def clear_edges(terms, domain):
    zero = jnp.zeros((SUB, LANES), jnp.float32)
    for comp in range(terms.shape[1]):
        terms[0, comp, 0:SUB, :] = zero
        terms[0, comp, SUB + domain:2 * SUB + domain, :] = zero


def run_layers(terms, smooth, table_ref, table_row, velocity_ref, shown_ref, own, width, reaches, domain):
    orders = terms.shape[0] - 1
    left, right = lane_weights()
    for layer, reach in enumerate(reaches):
        rows = min(domain, width + 2 * reach)
        start = jnp.minimum(jnp.maximum(own - reach, 0), domain - rows)
        start = pl.multiple_of(start, SUB)
        layer_step(terms, smooth, table_ref, table_row, velocity_ref, layer, start, rows, orders, None, left, right)
        for comp in range(terms.shape[1]):
            shown_ref[layer, comp] = terms[0, comp, pl.ds(pl.multiple_of(own, SUB), width + 2 * SUB), :]


def first_kernel(plan, table_ref, spot_ref, *refs):
    pieces, (field_ref, shown_ref, velocity_ref, terms, smooth) = refs[:plan.count], refs[plan.count:]
    clear_edges(terms, plan.domain)
    for number, piece in enumerate(pieces):
        at = pl.multiple_of(spot_ref[number] * plan.width, SUB)
        for comp in range(4):
            terms[0, comp, pl.ds(at + SUB, plan.width), :] = piece[comp]
        for layer in range(plan.layers):
            velocity_ref[layer, pl.ds(at, plan.width), :] = piece[4 + layer].astype(jnp.int32)
    own = spot_ref[plan.count] * plan.width
    run_layers(terms, smooth, table_ref, spot_ref[plan.count + 1], velocity_ref, shown_ref, own, plan.width,
               plan.reaches[0], plan.domain)
    for comp in range(4):
        field_ref[comp] = terms[0, comp, SUB:SUB + plan.domain, :]


def later_kernel(plan, tick, table_ref, spot_ref, velocity_ref, before_ref, *refs):
    pieces, (field_ref, shown_ref, terms, smooth) = refs[:plan.count], refs[plan.count:]
    clear_edges(terms, plan.domain)
    enters = spot_ref[plan.count + 2] == tick

    @pl.when(jnp.logical_not(enters))
    def _():
        for comp in range(4):
            terms[0, comp, SUB:SUB + plan.domain, :] = before_ref[comp]

    @pl.when(enters)
    def _():
        for number, piece in enumerate(pieces):
            at = pl.multiple_of(spot_ref[number] * plan.width, SUB)
            for comp in range(4):
                terms[0, comp, pl.ds(at + SUB, plan.width), :] = piece[comp]

    own = spot_ref[plan.count] * plan.width
    entered = spot_ref[plan.count + 2] <= tick
    table_row = jnp.where(entered, spot_ref[plan.count + 3], spot_ref[plan.count + 4])
    run_layers(terms, smooth, table_ref, table_row, velocity_ref, shown_ref, own, plan.width,
               plan.reaches[tick], plan.domain)
    if tick + 1 < plan.ticks:
        for comp in range(4):
            field_ref[comp] = terms[0, comp, SUB:SUB + plan.domain, :]
    else:
        for comp in range(4):
            field_ref[comp] = terms[0, comp, pl.ds(pl.multiple_of(own + SUB, SUB), plan.width), :]


def image_kernel(plan, count, has_base, offsets_ref, *refs):
    shown = refs[:count]
    base_ref = refs[count] if has_base else None
    image_ref = refs[-1]
    tiles = plan.width // SUB

    def one(index, carry):
        offset = offsets_ref[index]
        for layer in range(plan.layers):
            for tile in range(tiles):
                at = SUB + tile * SUB
                total = base_ref[layer, index, at - SUB:at, :] if has_base else None
                for ref in shown:
                    for part in range(2):
                        term = (ref[layer, part, pl.ds(at - offset, SUB), :]
                                * ref[layer, 2 + part, pl.ds(at + offset, SUB), :])
                        total = term if total is None else total + term
                image_ref[layer, index, at - SUB:at, :] = total
        return carry

    lax.fori_loop(0, offsets_ref.shape[0], one, 0)


class Plan:
    pass


def gathered(value, plan):
    if plan.everything:
        return [value] + [
            lax.ppermute(value, "strip", [(i, i ^ other) for i in range(plan.strips)])
            for other in range(1, plan.strips)
        ]
    whole = lax.all_gather(value, "strip")
    return [lax.dynamic_index_in_dim(whole, plan.first + number, 0, keepdims=False) for number in range(plan.count)]


def shifted(value, steps):
    count = lax.axis_size("depth")
    return lax.ppermute(value, "depth", [(i, (i + steps) % count) for i in range(count)])


def per_device(arrivals, feed, velocity_index, offsets, coef_table):
    plan = Plan()
    field = arrivals[0, 0]
    plan.width = field.shape[1]
    plan.layers = velocity_index.shape[0]
    plan.ticks = feed.shape[0] + 1
    plan.strips = lax.axis_size("strip")
    orders = coef_table.shape[1] - 1
    sections = lax.axis_size("depth")
    section = lax.axis_index("depth")
    strip = lax.axis_index("strip")
    last = plan.ticks - 1
    steps = plan.ticks * plan.layers
    side = -(-(orders * steps + SUB) // plan.width)
    plan.count = min(plan.strips, 2 * side + 1)
    plan.domain = plan.count * plan.width
    plan.everything = plan.count == plan.strips and plan.strips & (plan.strips - 1) == 0
    plan.first = jnp.clip(strip - side, 0, plan.strips - plan.count)
    plan.reaches = [
        [orders * (steps - tick * plan.layers - layer) + SUB for layer in range(plan.layers)]
        for tick in range(plan.ticks)
    ]
    size = coef_table.shape[1] * 2
    table = coef_table.reshape(coef_table.shape[0] * size, coef_table.shape[-1])
    table = jnp.pad(table, ((0, -table.shape[0] % SUB), (0, LANES - table.shape[1])))
    if plan.everything:
        places = jnp.arange(plan.count, dtype=jnp.int32) ^ strip
    else:
        places = jnp.arange(plan.count, dtype=jnp.int32)
    batch = sections - 1 + last - section
    extra = [strip - plan.first, (sections - 1 - section) * size, last - section,
             jnp.maximum(batch, 0) * size, jnp.maximum(batch - sections, 0) * size]
    lane = jnp.arange(len(extra), dtype=jnp.int32)
    tail = sum(jnp.where(lane == number, value, 0) for number, value in enumerate(extra))
    spots = jnp.concatenate([places, tail.astype(jnp.int32)])

    message = jnp.concatenate([field, velocity_index.astype(jnp.float32)], axis=0)
    pieces = gathered(message, plan)

    full = jax.ShapeDtypeStruct((4, plan.domain, LANES), jnp.float32)
    shown = jax.ShapeDtypeStruct((plan.layers, 4, plan.width + 2 * SUB, LANES), jnp.float32)
    levels = jax.ShapeDtypeStruct((plan.layers, plan.domain, LANES), jnp.int32)
    scratch = [pltpu.VMEM((orders + 1, 4, plan.domain + 2 * SUB, LANES), jnp.float32),
               pltpu.VMEM((4, plan.domain + 2 * SUB, LANES), jnp.float32)]
    cost = pl.CostEstimate(flops=100_000_000, bytes_accessed=4_000_000, transcendentals=0)
    field, shown_first, velocity = pl.pallas_call(
        functools.partial(first_kernel, plan),
        out_shape=(full, shown, levels),
        in_specs=[VMEM, SMEM] + [VMEM] * plan.count,
        out_specs=(VMEM,) * 3,
        scratch_shapes=scratch,
        cost_estimate=cost,
        name="first",
    )(table, spots, *pieces)
    moved = shifted(field, last)
    velocities = [shifted(velocity, last - tick) if tick < last else velocity for tick in range(1, plan.ticks)]
    own_feed = lax.dynamic_index_in_dim(feed, jnp.clip(last - 1 - section, 0, last - 1), 0, keepdims=False)[0]
    feeds = gathered(own_feed, plan)

    def imaged(parts, base):
        image = jax.ShapeDtypeStruct((plan.layers, offsets.shape[0], plan.width, LANES), jnp.float32)
        extra = () if base is None else (base,)
        return pl.pallas_call(
            functools.partial(image_kernel, plan, len(parts), base is not None),
            out_shape=image,
            in_specs=[SMEM] + [VMEM] * (len(parts) + len(extra)),
            out_specs=VMEM,
            cost_estimate=pl.CostEstimate(flops=10_000_000, bytes_accessed=2_000_000, transcendentals=0),
            name="image",
        )(offsets, *parts, *extra)

    image = imaged([shown_first], None)
    parts = []
    for tick in range(1, plan.ticks):
        out = full if tick < last else jax.ShapeDtypeStruct((4, plan.width, LANES), jnp.float32)
        moved, seen = pl.pallas_call(
            functools.partial(later_kernel, plan, tick),
            out_shape=(out, shown),
            in_specs=[VMEM, SMEM, VMEM, VMEM] + [VMEM] * plan.count,
            out_specs=(VMEM,) * 2,
            scratch_shapes=scratch,
            cost_estimate=cost,
            name=f"later{tick}",
        )(table, spots, velocities[tick - 1], moved, *feeds)
        parts.append(seen if tick == last else shifted(seen, tick - last))
    image = imaged(parts, image)
    return image, moved[None, None]


def solution(mesh):
    placed = (
        P("depth", None, None, "strip", None),
        P(None, None, None, "strip", None),
        P("depth", "strip", None),
        P(),
        P(),
    )
    return jax.shard_map(
        per_device,
        mesh=mesh,
        in_specs=placed,
        out_specs=(P("depth", None, "strip", None), P("depth", None, None, "strip", None)),
        check_vma=False,
    )
```

```python
import functools

import jax
import jax.numpy as jnp
from jax import lax
from jax.experimental import pallas as pl
from jax.experimental.pallas import tpu as pltpu
from jax.sharding import PartitionSpec as P


SUB = 8
LANES = 128
PAIR = 2
VMEM = pl.BlockSpec(memory_space=pltpu.VMEM)
SMEM = pl.BlockSpec(memory_space=pltpu.SMEM)


def tile_at(start):
    return pl.ds(pl.multiple_of(start, SUB), SUB)


def picked(table_ref, row, index):
    row = jnp.broadcast_to(table_ref[pl.ds(row, 1), :], (SUB, LANES))
    return jnp.take_along_axis(row, index, axis=1, mode="promise_in_bounds")


def layer_step(terms, smooth, total, sets, early, layer, start, rows, orders, left, right):
    tiles = rows // SUB
    comps = terms.shape[1]
    zero = jnp.zeros((SUB, LANES), jnp.float32)
    base = start + SUB
    for comp in range(comps):
        smooth[comp, 0:SUB, :] = zero
        smooth[comp, SUB + rows:2 * SUB + rows, :] = zero

    def products(get, order, cells):
        re, im = get(2 * order), get(2 * order + 1)
        a, b = cells[:PAIR]
        pieces = [re * a - im * b, re * b + im * a]
        if len(cells) > PAIR:
            a, b = cells[PAIR:]
            pieces += [re * a + im * b, re * b - im * a]
        return pieces

    for order in range(orders):
        held = {}

        def along_y(tile):
            cells = [terms[order, comp, tile_at(base + tile * SUB), :] for comp in range(comps)]
            for comp in range(comps):
                sides = left * pltpu.roll(cells[comp], 1, 1) + right * pltpu.roll(cells[comp], LANES - 1, 1)
                smooth[comp, SUB + tile * SUB:2 * SUB + tile * SUB, :] = cells[comp] + sides
                held[tile, comp] = sides - cells[comp]
            if early and order == 0:
                for comp, piece in enumerate(products(sets(layer, tile, start), 0, cells)):
                    total[comp, tile * SUB:tile * SUB + SUB, :] = piece

        def along_x(tile):
            low = SUB + tile * SUB
            found = []
            for comp in range(comps):
                sides = smooth[comp, low - 1:low - 1 + SUB, :] + smooth[comp, low + 1:low + 1 + SUB, :]
                following = held.pop((tile, comp)) + 0.5 * sides
                if order == 0:
                    following = 0.5 * following
                else:
                    following = following - terms[order - 1, comp, tile_at(base + tile * SUB), :]
                if not early or order + 1 < orders:
                    terms[order + 1, comp, tile_at(base + tile * SUB), :] = following
                found.append(following)
            if early:
                pieces = products(sets(layer, tile, start), order + 1, found)
                for comp, piece in enumerate(pieces):
                    value = total[comp, tile * SUB:tile * SUB + SUB, :] + piece
                    if order + 1 < orders:
                        total[comp, tile * SUB:tile * SUB + SUB, :] = value
                    else:
                        terms[0, comp, tile_at(base + tile * SUB), :] = value

        for tile in range(tiles + 1):
            if tile < tiles:
                along_y(tile)
            if tile > 0:
                along_x(tile - 1)
    if early:
        return
    for tile in range(tiles):
        sums = None
        get = sets(layer, tile, start)
        for order in range(orders + 1):
            pieces = products(get, order, [terms[order, comp, tile_at(base + tile * SUB), :] for comp in range(comps)])
            sums = pieces if sums is None else [old + piece for old, piece in zip(sums, pieces)]
        for comp in range(comps):
            terms[0, comp, tile_at(base + tile * SUB), :] = sums[comp]


def looked_up(table_ref, table_row, velocity_ref):
    def sets(layer, tile, start):
        index = velocity_ref[layer, tile_at(start + tile * SUB), :]
        return lambda number: picked(table_ref, table_row + number, index)

    return sets


def stored(sets_ref):
    def sets(layer, tile, start):
        return lambda number: sets_ref[layer, number, tile * SUB:tile * SUB + SUB, :]

    return sets


def close_start(plan, own):
    reach, rows = plan.close[0]
    return jnp.clip(own - reach, 0, plan.domain - rows)


def sets_kernel(plan, tick, table_ref, spot_ref, velocity_ref, sets_ref):
    pair, own = spot_ref[plan.count] * plan.width, spot_ref[plan.count + 1] * plan.width
    row = spot_ref[plan.count + 3 + tick]
    last = tick + 1 == plan.ticks
    for layer, (reach, rows) in enumerate(plan.close if last else plan.windows[tick]):
        if last:
            outer = close_start(plan, own)
            start = outer + jnp.clip(own - outer - reach, 0, plan.close[0][1] - rows)
        else:
            start = jnp.clip(pair - reach, 0, plan.domain - rows)
        for tile in range(rows // SUB):
            index = velocity_ref[layer, tile_at(start + tile * SUB), :]
            for number in range(2 * plan.orders + 2):
                sets_ref[layer, number, tile * SUB:tile * SUB + SUB, :] = picked(table_ref, row + number, index)


def run_layers(plan, tick, terms, smooth, total, sets, early, spot_ref, mine_ref, theirs_ref):
    left, right = lane_weights()
    pair, mine, theirs = [spot_ref[plan.count + number] * plan.width for number in range(3)]
    for layer, (reach, rows) in enumerate(plan.windows[tick]):
        start = pl.multiple_of(jnp.clip(pair - reach, 0, plan.domain - rows), SUB)
        layer_step(terms, smooth, total, sets, early, layer, start, rows, plan.orders, left, right)
        for comp in range(PAIR):
            for at, ref in ((mine, mine_ref), (theirs, theirs_ref)):
                ref[layer, comp] = terms[0, comp, pl.ds(pl.multiple_of(at, SUB), plan.width + 2 * SUB), :]


def lane_weights():
    lane = lax.broadcasted_iota(jnp.int32, (SUB, LANES), 1)
    left = jnp.where(lane == 0, 0.0, 0.5).astype(jnp.float32)
    right = jnp.where(lane == LANES - 1, 0.0, 0.5).astype(jnp.float32)
    return left, right


def clear_edges(terms, domain):
    zero = jnp.zeros((SUB, LANES), jnp.float32)
    for comp in range(terms.shape[1]):
        terms[0, comp, 0:SUB, :] = zero
        terms[0, comp, SUB + domain:2 * SUB + domain, :] = zero


def put_window(plan, terms, spot_ref, tick, field_ref):
    reach, rows = plan.windows[tick][0]
    start = jnp.clip(spot_ref[plan.count] * plan.width - reach, 0, plan.domain - rows)
    for comp in range(PAIR):
        field_ref[comp] = terms[0, comp, pl.ds(pl.multiple_of(start + SUB, SUB), rows), :]


def put_pieces(plan, terms, spot_ref, pieces, firsts):
    for number, (piece, first) in enumerate(zip(pieces, firsts)):
        at = pl.multiple_of(spot_ref[number] * plan.width, SUB)
        for comp in range(PAIR):
            terms[0, comp, pl.ds(at + SUB, plan.width), :] = piece[first + comp]


def first_kernel(plan, table_ref, spot_ref, *refs):
    pieces, rest = refs[:plan.count], refs[plan.count:]
    field_ref, mine_ref, theirs_ref, velocity_ref, terms, smooth, total = rest
    clear_edges(terms, plan.domain)
    put_pieces(plan, terms, spot_ref, pieces, [first for first, _, _ in plan.firsts])
    for number, piece in enumerate(pieces):
        at = pl.multiple_of(spot_ref[number] * plan.width, SUB)
        for layer in range(plan.layers):
            velocity_ref[layer, pl.ds(at, plan.width), :] = piece[plan.firsts[number][1] + layer].astype(jnp.int32)
    sets = looked_up(table_ref, spot_ref[plan.count + 3], velocity_ref)
    run_layers(plan, 0, terms, smooth, total, sets, False, spot_ref, mine_ref, theirs_ref)
    put_window(plan, terms, spot_ref, 1, field_ref)


def later_kernel(plan, tick, entry, leave, ready, spot_ref, before_ref, *refs):
    sources, refs = refs[:2 - ready], refs[2 - ready:]
    pieces, rest = refs[:plan.count], refs[plan.count:]
    mine_ref, theirs_ref, terms, smooth, total = rest[-5:]
    clear_edges(terms, plan.domain)
    section = spot_ref[plan.count + 8]
    reach, rows = plan.windows[tick][0]
    start = jnp.clip(spot_ref[plan.count] * plan.width - reach, 0, plan.domain - rows)
    for comp in range(PAIR):
        terms[0, comp, pl.ds(pl.multiple_of(start + SUB, SUB), rows), :] = before_ref[comp]
    feeds = [first for _, _, first in plan.firsts]
    if entry is not None:
        pl.when(section == entry)(lambda: put_pieces(plan, terms, spot_ref, pieces, feeds))
    sets = stored(*sources) if ready else looked_up(sources[0], spot_ref[plan.count + 3 + tick], sources[1])
    run_layers(plan, tick, terms, smooth, total, sets, ready, spot_ref, mine_ref, theirs_ref)
    if leave is not None:
        pl.when(section == leave)(lambda: put_pieces(plan, terms, spot_ref, pieces, feeds))
    if tick + 2 < plan.ticks:
        put_window(plan, terms, spot_ref, tick + 1, rest[0])
        return
    for number, ref in ((1, rest[0]), (2, rest[1])):
        start = close_start(plan, spot_ref[plan.count + number] * plan.width)
        for comp in range(PAIR):
            ref[comp] = terms[0, comp, pl.ds(pl.multiple_of(start + SUB, SUB), plan.close[0][1]), :]


def last_kernel(plan, spot_ref, sets_ref, near_ref, cross_ref, mine_ref, theirs_ref, terms, smooth, total):
    rows = plan.close[0][1]
    clear_edges(terms, rows)
    for comp in range(PAIR):
        terms[0, comp, SUB:SUB + rows, :] = near_ref[comp]
        terms[0, PAIR + comp, SUB:SUB + rows, :] = cross_ref[comp]
    own = spot_ref[plan.count + 1] * plan.width
    own = own - close_start(plan, own)
    left, right = lane_weights()
    for layer, (reach, inner) in enumerate(plan.close):
        start = pl.multiple_of(jnp.clip(own - reach, 0, rows - inner), SUB)
        layer_step(terms, smooth, total, stored(sets_ref), True, layer, start, inner, plan.orders, left, right)
        for comp in range(PAIR):
            at = pl.ds(pl.multiple_of(own, SUB), plan.width + 2 * SUB)
            mine_ref[layer, comp] = terms[0, comp, at, :]
            theirs_ref[layer, comp] = terms[0, PAIR + comp, at, :]


def image_kernel(plan, ticks, has_base, ends, group, spot_ref, offsets_ref, *refs):
    mine, theirs = refs[:ticks], refs[ticks:2 * ticks]
    base_ref = refs[2 * ticks] if has_base else None
    image_ref = refs[2 * ticks + has_base]
    role = spot_ref[plan.count + 7]
    sign = 1 - 2 * role
    tiles = plan.width // SUB
    step = pl.program_id(0)

    def one(index, carry):
        offset = offsets_ref[step * group + index] * sign
        for layer in range(plan.layers):
            for tile in range(tiles):
                at = SUB + tile * SUB
                total = base_ref[layer, index, at - SUB:at, :] if has_base else None
                for own, other in zip(mine, theirs):
                    for part in range(PAIR):
                        term = own[layer, part, pl.ds(at - offset, SUB), :] * other[layer, part, pl.ds(at + offset, SUB), :]
                        total = term if total is None else total + term
                image_ref[layer, index, at - SUB:at, :] = total
        return carry

    lax.fori_loop(0, group, one, 0, unroll=2)
    if ends:
        out_ref = refs[-1]

        @pl.when(step == 0)
        def _():
            for comp in range(PAIR):
                out_ref[PAIR * role + comp] = mine[-1][plan.layers - 1, comp, SUB:SUB + plan.width, :]
                out_ref[PAIR * (1 - role) + comp] = theirs[-1][plan.layers - 1, comp, SUB:SUB + plan.width, :]


class Plan:
    pass


def shifted(value, steps, swap=False):
    return moved_by(value, steps, swap)


def moved_by(value, steps, swap):
    sections, strips = lax.axis_size("depth"), lax.axis_size("strip")
    if steps == 0:
        return lax.ppermute(value, "strip", [(i, i ^ 1) for i in range(strips)])
    if not swap:
        return lax.ppermute(value, "depth", [(i, (i + steps) % sections) for i in range(sections)])
    pairs = [(i * strips + k, ((i + steps) % sections) * strips + (k ^ 1)) for i in range(sections) for k in range(strips)]
    return lax.ppermute(value, ("depth", "strip"), pairs)


def per_device(arrivals, feed, velocity_index, offsets, coef_table):
    plan = Plan()
    field = arrivals[0, 0]
    plan.width = width = field.shape[1]
    plan.layers = velocity_index.shape[0]
    plan.ticks = feed.shape[0] + 1
    plan.orders = coef_table.shape[1] - 1
    strips = lax.axis_size("strip")
    sections = lax.axis_size("depth")
    section = lax.axis_index("depth")
    strip = lax.axis_index("strip")
    role = strip % 2
    last = plan.ticks - 1
    steps = plan.ticks * plan.layers
    side = -(-(plan.orders * steps + SUB) // width)
    plan.count = count = min(strips, 2 * side + 2)
    plan.domain = count * width
    everything = count == strips and strips & (strips - 1) == 0
    first = jnp.clip(strip - role - side, 0, strips - count)

    def window(step):
        reach = plan.orders * (steps - step) + SUB
        spans = [min(strips * width, (pair + 2) * width + reach) - max(0, pair * width - reach) for pair in range(0, strips, 2)]
        return reach, min(plan.domain, max(spans))

    plan.windows = [[window(tick * plan.layers + layer) for layer in range(plan.layers)] for tick in range(plan.ticks)]

    plan.close = []
    for layer in range(plan.layers):
        reach = plan.orders * (plan.layers - layer) + SUB
        plan.close.append((reach, min(plan.domain, width + 2 * reach)))
    size = coef_table.shape[1] * 2
    table = coef_table.reshape(coef_table.shape[0] * size, coef_table.shape[-1])
    odd = (jnp.arange(table.shape[0], dtype=jnp.int32) % 2 == 1)[:, None]
    table = jnp.where(jnp.logical_and(odd, role == 1), -table, table)
    table = jnp.pad(table, ((0, -table.shape[0] % SUB), (0, LANES - table.shape[1])))
    places = jnp.arange(count, dtype=jnp.int32)
    if everything:
        places = places ^ strip
    rows = [sections - 1 - section, sections - section,
            jnp.where(section == sections - 1, sections + 1, sections - section), sections + 2 - section]
    extra = [strip - role - first, strip - first, (strip ^ 1) - first] + [row * size for row in rows] + [role, section]
    lane = jnp.arange(count + len(extra), dtype=jnp.int32)
    spots = jnp.where(lane < count, jnp.pad(places, (0, len(extra))), 0)
    for number, value in enumerate(extra):
        spots = jnp.where(lane == count + number, value, spots)
    spots = spots.astype(jnp.int32)

    own_feed = lax.dynamic_index_in_dim(feed, jnp.minimum((sections - section) % sections, last - 1), 0, keepdims=False)[0]
    levels = velocity_index.astype(jnp.float32)

    def halves(value):
        return jnp.where(role == 1, value[PAIR:], value[:PAIR]), jnp.where(role == 1, value[:PAIR], value[PAIR:])

    if everything:
        ours, others = halves(field)
        fed = halves(own_feed)
        joined = jnp.concatenate([fed[0], ours, levels, others, fed[1]], axis=0)
        sent = [joined[:2 * PAIR + plan.layers], joined[2 * PAIR:]]
        pieces = [sent[0]]
        near, far = (PAIR, 2 * PAIR, 0), (plan.layers, 0, plan.layers + PAIR)
        plan.firsts = [near] + [near if j % 2 == 0 else far for j in range(1, strips)]
        for j in range(1, strips):
            pairs = [(i, i ^ j) for i in range(strips)]
            pieces.append(lax.ppermute(sent[j % 2], "strip", pairs))
    else:
        plan.firsts = [(0, PAIR, PAIR + plan.layers)] * count
        whole = lax.all_gather(jnp.concatenate([field, levels, own_feed], axis=0), "strip")
        pieces = []
        for number in range(count):
            piece = lax.dynamic_index_in_dim(whole, first + number, 0, keepdims=False)
            low, mid = PAIR * 2, PAIR * 2 + plan.layers
            pieces.append(jnp.concatenate([halves(piece[:low])[0], piece[low:mid], halves(piece[mid:])[0]], axis=0))

    shown = jax.ShapeDtypeStruct((plan.layers, PAIR, width + 2 * SUB, LANES), jnp.float32)
    grid_levels = jax.ShapeDtypeStruct((plan.layers, plan.domain, LANES), jnp.int32)
    padded = plan.domain + 2 * SUB
    scratch = [pltpu.VMEM((plan.orders + 1, PAIR, padded, LANES), jnp.float32),
               pltpu.VMEM((PAIR, padded, LANES), jnp.float32),
               pltpu.VMEM((PAIR, plan.domain, LANES), jnp.float32)]
    row = LANES * 4
    grant = row * (PAIR * padded * (plan.orders + 3) + 2 * plan.domain * (2 * PAIR + plan.layers)
                   + count * width * (2 * PAIR + plan.layers) + 4 * plan.layers * PAIR * (width + 2 * SUB)
                   + table.shape[0] + plan.layers * size * plan.domain) + (2 << 20)
    params = pltpu.CompilerParams(vmem_limit_bytes=grant)
    cost = pl.CostEstimate(flops=100_000_000, bytes_accessed=4_000_000, transcendentals=0)

    def part(tick):
        return jax.ShapeDtypeStruct((PAIR, plan.windows[tick][0][1], LANES), jnp.float32)

    def all_sets(tick, velocity):
        rows = max(rows for _, rows in (plan.close if tick == last else plan.windows[tick]))
        return pl.pallas_call(
            functools.partial(sets_kernel, plan, tick),
            out_shape=jax.ShapeDtypeStruct((plan.layers, size, rows, LANES), jnp.float32),
            in_specs=[VMEM, SMEM, VMEM],
            out_specs=VMEM,
            compiler_params=pltpu.CompilerParams(vmem_limit_bytes=grant),
            cost_estimate=pl.CostEstimate(flops=10_000_000, bytes_accessed=2_000_000, transcendentals=0),
        )(table, spots, velocity)

    close = jax.ShapeDtypeStruct((PAIR, plan.close[0][1], LANES), jnp.float32)

    def run(tick, moved, sources, entry=None, leave=None):
        outs = (part(tick + 1),) if tick + 1 < last else (close, close)
        return pl.pallas_call(
            functools.partial(later_kernel, plan, tick, entry, leave, len(sources) == 1),
            out_shape=outs + (shown, shown),
            in_specs=[SMEM] + [VMEM] * (1 + len(sources) + count),
            out_specs=(VMEM,) * (len(outs) + 2),
            scratch_shapes=scratch,
            compiler_params=params,
            cost_estimate=cost,
        )(spots, moved, *sources, *pieces)

    def run_last(sets, near, cross):
        rows = plan.close[0][1]
        return pl.pallas_call(
            functools.partial(last_kernel, plan),
            out_shape=(shown, shown),
            in_specs=[SMEM] + [VMEM] * 3,
            out_specs=(VMEM,) * 2,
            scratch_shapes=[pltpu.VMEM((plan.orders + 1, 2 * PAIR, rows + 2 * SUB, LANES), jnp.float32),
                            pltpu.VMEM((2 * PAIR, rows + 2 * SUB, LANES), jnp.float32),
                            pltpu.VMEM((2 * PAIR, rows, LANES), jnp.float32)],
            compiler_params=params,
            cost_estimate=cost,
            name="last",
        )(spots, sets, near, cross)

    start = pl.pallas_call(
        functools.partial(first_kernel, plan),
        out_shape=(part(1), shown, shown, grid_levels),
        in_specs=[VMEM, SMEM] + [VMEM] * count,
        out_specs=(VMEM,) * 4,
        scratch_shapes=scratch,
        compiler_params=params,
        cost_estimate=cost,
        name="first",
    )
    moved, mine, theirs, velocity = start(table, spots, *pieces)

    def imaged(ticks, base, ends):
        group = offsets.shape[0] // 2 if ends and offsets.shape[0] % 2 == 0 else offsets.shape[0]
        image = jax.ShapeDtypeStruct((plan.layers, offsets.shape[0], width, LANES), jnp.float32)
        block = pl.BlockSpec((plan.layers, group, width, LANES), lambda i: (0, i, 0, 0))
        whole = pl.BlockSpec(shown.shape, lambda i: (0, 0, 0, 0))
        out = jax.ShapeDtypeStruct((2 * PAIR, width, LANES), jnp.float32)
        outs, specs = [image], [block]
        if ends:
            outs, specs = [image, out], [block, pl.BlockSpec(out.shape, lambda i: (0, 0, 0))]
        operands = [mine for mine, _ in ticks] + [theirs for _, theirs in ticks]
        return pl.pallas_call(
            functools.partial(image_kernel, plan, len(ticks), base is not None, ends, group),
            grid=(offsets.shape[0] // group,),
            out_shape=outs,
            in_specs=[SMEM, SMEM] + [whole] * len(operands) + ([block] if base is not None else []),
            out_specs=specs,
            compiler_params=pltpu.CompilerParams(vmem_limit_bytes=8 << 20),
            cost_estimate=pl.CostEstimate(flops=10_000_000, bytes_accessed=2_000_000, transcendentals=0),
            name="image",
        )(spots, offsets, *operands, *(() if base is None else (base,)))

    moved, nearer = shifted(moved, 1), shifted(velocity, -1)
    first_theirs = shifted(theirs, 0)
    moved, sets = lax.optimization_barrier((moved, all_sets(1, velocity)))
    parts = [(mine, first_theirs)]
    moved, mine, theirs = run(1, moved, (sets,), entry=0)
    near, cross, away, beyond = run(2, moved, (table, nearer), entry=sections - 1, leave=sections - 2)
    away, velocity = lax.optimization_barrier((away, velocity))
    near, cross = shifted(near, 2), shifted(cross, 2, True)
    parts.append((mine, shifted(theirs, 0)))
    image, = imaged(parts, None, False)
    away, beyond = shifted(away, 1), shifted(beyond, 1, True)
    near, cross, image, sets = lax.optimization_barrier((near, cross, image, all_sets(3, velocity)))
    mine, theirs = run_last(sets, near, cross)
    image, outflow = imaged([(away, beyond), (mine, theirs)], image, True)
    return image, outflow[None, None]


def solution(mesh):
    placed = (
        P("depth", None, None, "strip", None),
        P(None, None, None, "strip", None),
        P("depth", "strip", None),
        P(),
        P(),
    )
    return jax.shard_map(
        per_device,
        mesh=mesh,
        in_specs=placed,
        out_specs=(P("depth", None, "strip", None), P("depth", None, None, "strip", None)),
        check_vma=False,
    )
```
